32 devices in a mesh: grp: 1, row: 32 (over z, y, x, core).
Axes of the slice: x: 2, y: 2, z: 4, core: 2. Of those that a mesh axis runs over, the one named last changes fastest.
Arguments:
- homolog_matrix: bfloat16 [64, 128, 256], P(('grp', 'row')), may hold values from -6 to 6
- alignment_mask: int32 [64, 128], P(('grp', 'row')), may hold values from 0 to 1, as said below
- pair_state_input: bfloat16 [128, 128, 128], P(('grp', 'row')), may hold values from -3 to 3
- chain_label: int32 [128], P('grp'), may hold values from 0 to 3, never falling along the last dimension, each value on 1 to 64 neighbouring positions
- residue_number_index: int32 [128], P('grp'), may hold values from 1 to 382, as said below
- relative_position_table: float32 [66, 128], replicated, may hold values from -3 to 3
- tensor_factor_coefficients: bfloat16 [256, 64], replicated, may hold values from -0.375 to 0.375
- outer_output_weight: bfloat16 [1024, 128], replicated, may hold values from -3 to 3
- scorer_entry_coefficients: bfloat16 [256, 1024], replicated, may hold values from -0.375 to 0.375
- scorer_final_coefficients: bfloat16 [256, 256], replicated, may hold values from -0.375 to 0.375
- pair_bias_weight: bfloat16 [128, 8], replicated
- triangle_input_weight: bfloat16 [128, 512], replicated, may hold values from -0.5 to 0.5
- triangle_output_gate: bfloat16 [128, 128], replicated, may hold values from -1.5 to 1.5
- triangle_output_weight: bfloat16 [128, 128], replicated, may hold values from -1.796875 to 1.796875
Outputs:
- homolog_revised: bfloat16 [64, 128, 256], P(('grp', 'row'))
- pair_state_output: bfloat16 [128, 128, 128], P(('grp', 'row'))
The draws below stay inside these ranges and needn't reach their ends.
Inputs may be any that keep to these rules, and one draw needn't show every extreme that they name: `alignment_mask`: 1 marks a live entry of an MSA row. `chain_label`: chain ids never fall along the residues; a chain holds at most 64 residues. `residue_number_index`: residue numbers strictly increase along the residues.
All inputs are finite; a program needn't handle non-finite values.
Results may differ from the reference program's by a relative error of at most 0.03.
Values may be sent and summed in bfloat16 or wider, within the bound.
A program may use at most 128 MiB of HBM per device.

```python
import math
import jax
import jax.numpy as jnp
import numpy as np
from jax import lax

RES_DEV = 4
HOMOLOG_FEATS = 256
CZ = 128
SCORER_GROUPS = 8
SCORER_SPAN = 32
TENSOR_FEATS = 32
TRI_C = 128
REL_MAX = 32
CHAINS = 4
BINS = 66
HOMOLOG_LINES = 64
AMINO_SITES = 128
N_ROW = 32


def draw_alignment_mask(key, part):
    uniform_ints = jax.random.randint(key, (HOMOLOG_LINES, AMINO_SITES), 0, 1000)
    row_ids = jnp.arange(HOMOLOG_LINES, dtype=jnp.int32)[:, None]
    thresholds = 300 + 650 * row_ids // max(HOMOLOG_LINES - 1, 1)
    return (uniform_ints < thresholds).astype(jnp.int32)


def draw_residue_number_index(key, part):
    positions = jnp.arange(AMINO_SITES, dtype=jnp.int32)
    increments = jax.random.randint(key, (AMINO_SITES,), 1, 4).astype(jnp.int32)
    increments = jnp.where(positions == 0, 1, increments).astype(jnp.int32)
    numbers = jnp.cumsum(increments).astype(jnp.int32)
    return jnp.where(positions == AMINO_SITES - 1, 3 * AMINO_SITES - 2, numbers).astype(jnp.int32)


def draw_pair_bias_weight(key, part):
    normal_part = jax.random.normal(key, (CZ, SCORER_GROUPS), jnp.float32) / math.sqrt(CZ)
    return normal_part.astype(jnp.bfloat16)


def steps_of(stream_key, dims, cuts, smallest, high):
    factor_of = 1.0
    for axis_at, parts in cuts:
        steps = jax.random.uniform(jax.random.fold_in(jax.random.fold_in(stream_key, 6), axis_at), (parts,), jnp.float32, smallest / len(cuts), high / len(cuts))
        factor_of = factor_of * jnp.repeat(jnp.exp(steps), dims[axis_at] // parts).reshape((-1,) + (1,) * (len(dims) - 1 - axis_at))
    return factor_of


def length_profile(count, total, bound, slope):
    loads = [(1 << 20) // math.isqrt(rank ** slope) + 1 for rank in range(2, count + 1)]
    rest, given = total - bound - (count - 1), [1] * (count - 1)
    while rest > 0:
        movable = [i for i in range(count - 1) if given[i] < bound]
        pool, remaining = sum([loads[i] for i in movable]), rest
        for i in movable:
            extra = min(bound - given[i], max(1, remaining * loads[i] // pool), rest)
            given[i] = given[i] + extra
            rest = rest - extra
    return np.array([bound] + given)


def uneven_parts(rng, count, total, bound, slope):
    if count == 2:
        one = jax.random.randint(rng, (), max(1, total - bound), min(bound, total - 1) + 1)
        return jnp.stack([one, total - one])
    sizes = jnp.asarray(length_profile(count, total, bound, slope), jnp.int32)
    couples = (count - 1) // 2
    source_of, taker = sizes[1:1 + 2 * couples:2], sizes[2:2 + 2 * couples:2]
    room = jnp.minimum(source_of - 1, bound - taker)
    passed = jax.random.randint(jax.random.fold_in(rng, 1), (couples,), 0, 1 << 20) % (room + 1)
    sizes = sizes.at[1:1 + 2 * couples:2].set(source_of - passed).at[2:2 + 2 * couples:2].set(taker + passed)
    return sizes[jax.random.permutation(jax.random.fold_in(rng, 2), count)]


def normal_values(rng, dims, width, bound, pieces=(), kind=jnp.bfloat16):
    entries = jax.random.normal(rng, dims, jnp.float32) * width
    if len(pieces) > 0:
        entries = steps_of(rng, dims, pieces, -0.22, 0.18) * entries
    return jnp.clip(entries, min=-bound, max=bound).astype(kind)


def setup_inputs(seed: int = 0, part: int = 0) -> dict:
    seeds = jax.random.split(jax.random.key(seed), 15)
    part_keys = jax.random.split(jax.random.fold_in(seeds[14], part), 15)
    homolog_matrix = normal_values(part_keys[0], (HOMOLOG_LINES, AMINO_SITES, HOMOLOG_FEATS), 1.0, 6.0, ((0, 32),))
    alignment_mask = draw_alignment_mask(jax.random.fold_in(jax.random.fold_in(seeds[14], part), 71), part)
    pair_state_input = normal_values(part_keys[2], (AMINO_SITES, AMINO_SITES, CZ), 0.5, 3.0, ((0, 32),))
    chain_label = jnp.searchsorted(jnp.cumsum(uneven_parts(part_keys[3], CHAINS, AMINO_SITES, AMINO_SITES // 2, 0)), jnp.arange(AMINO_SITES), side="right").astype(jnp.int32)
    residue_number_index = draw_residue_number_index(jax.random.fold_in(jax.random.fold_in(seeds[14], part), 71), part)
    relative_position_table = normal_values(seeds[5], (BINS, CZ), 0.5, 3.0, (), jnp.float32)
    tensor_factor_coefficients = normal_values(seeds[6], (HOMOLOG_FEATS, 2 * TENSOR_FEATS), HOMOLOG_FEATS ** -0.5, 0.375)
    outer_output_weight = normal_values(seeds[7], (TENSOR_FEATS * TENSOR_FEATS, CZ), 0.5, 3.0)
    scorer_entry_coefficients = normal_values(seeds[8], (HOMOLOG_FEATS, 4 * HOMOLOG_FEATS), HOMOLOG_FEATS ** -0.5, 0.375)
    scorer_final_coefficients = normal_values(seeds[9], (HOMOLOG_FEATS, HOMOLOG_FEATS), HOMOLOG_FEATS ** -0.5, 0.375)
    pair_bias_weight = draw_pair_bias_weight(jax.random.fold_in(seeds[14], 71), part)
    triangle_input_weight = normal_values(seeds[11], (CZ, 4 * TRI_C), CZ ** -0.5, 0.5)
    triangle_output_gate = normal_values(seeds[12], (CZ, CZ), 0.25, 1.5)
    triangle_output_weight = normal_values(seeds[13], (TRI_C, CZ), 0.3, 1.796875)
    return dict(homolog_matrix=homolog_matrix, alignment_mask=alignment_mask, pair_state_input=pair_state_input, chain_label=chain_label, residue_number_index=residue_number_index, relative_position_table=relative_position_table, tensor_factor_coefficients=tensor_factor_coefficients, outer_output_weight=outer_output_weight, scorer_entry_coefficients=scorer_entry_coefficients, scorer_final_coefficients=scorer_final_coefficients, pair_bias_weight=pair_bias_weight, triangle_input_weight=triangle_input_weight, triangle_output_gate=triangle_output_gate, triangle_output_weight=triangle_output_weight)


def layer_normalize(values):
    centre = lax.optimization_barrier(jnp.mean(values, axis=-1, keepdims=True))
    shifted = values - centre
    spread = lax.optimization_barrier(jnp.mean(shifted * shifted, axis=-1, keepdims=True))
    return shifted * lax.rsqrt(spread + 1e-05)

def reference(homolog_matrix, alignment_mask, pair_state_input, chain_label, residue_number_index, relative_position_table, tensor_factor_coefficients, outer_output_weight, scorer_entry_coefficients, scorer_final_coefficients, pair_bias_weight, triangle_input_weight, triangle_output_gate, triangle_output_weight):
    active_entry_mask = alignment_mask.astype(jnp.float32)
    homolog_rescaled = layer_normalize(homolog_matrix.astype(jnp.float32)).astype(jnp.bfloat16)
    homolog_lines_merged = homolog_rescaled.reshape(HOMOLOG_LINES * AMINO_SITES, HOMOLOG_FEATS)
    projected_rows = jnp.dot(homolog_lines_merged, tensor_factor_coefficients, preferred_element_type=jnp.float32).reshape(HOMOLOG_LINES, AMINO_SITES, 2 * TENSOR_FEATS)
    left_factor = (projected_rows[..., :TENSOR_FEATS] * active_entry_mask[..., None]).astype(jnp.bfloat16)
    right_factor = (projected_rows[..., TENSOR_FEATS:] * active_entry_mask[..., None]).astype(jnp.bfloat16)
    right_wide = right_factor.astype(jnp.float32)

    def outer_block(block_index):
        row_start = (block_index * RES_DEV).astype(jnp.int32)
        left_block = lax.dynamic_slice_in_dim(left_factor, row_start, RES_DEV, 1).astype(jnp.float32)
        live_block = lax.dynamic_slice_in_dim(active_entry_mask, row_start, RES_DEV, 1)
        outer_sum = jnp.einsum('sic,sje->ijce', left_block, right_wide, precision=lax.Precision.HIGHEST)
        outer_flat = outer_sum.astype(jnp.bfloat16).reshape(RES_DEV * AMINO_SITES, TENSOR_FEATS * TENSOR_FEATS)
        pair_count = jnp.dot(live_block.T, active_entry_mask, precision=lax.Precision.HIGHEST)
        update = jnp.dot(outer_flat, outer_output_weight, preferred_element_type=jnp.float32).reshape(RES_DEV, AMINO_SITES, CZ)
        return update / (0.001 + pair_count[..., None])
    opm_update = lax.map(outer_block, jnp.arange(N_ROW, dtype=jnp.int32)).reshape(AMINO_SITES, AMINO_SITES, CZ)
    same_chain = chain_label[:, None] == chain_label[None, :]
    offsets = jnp.clip(residue_number_index[:, None] - residue_number_index[None, :], -REL_MAX, REL_MAX) + REL_MAX
    bin_index = jnp.where(same_chain, offsets, 2 * REL_MAX + 1).astype(jnp.int32)
    position_term = relative_position_table[bin_index]
    updated = (pair_state_input.astype(jnp.float32) + position_term + opm_update).astype(jnp.bfloat16)
    pair_norm = layer_normalize(updated.astype(jnp.float32)).astype(jnp.bfloat16)
    pair_flat = pair_norm.reshape(AMINO_SITES * AMINO_SITES, CZ)
    head_bias = jnp.dot(pair_flat, pair_bias_weight, preferred_element_type=jnp.float32).astype(jnp.bfloat16)
    head_bias = head_bias.reshape(AMINO_SITES, AMINO_SITES, SCORER_GROUPS).transpose(2, 0, 1)
    tri_projected = jnp.dot(pair_flat, triangle_input_weight, preferred_element_type=jnp.float32)
    tri_left = (jax.nn.sigmoid(tri_projected[:, :TRI_C]) * tri_projected[:, TRI_C:2 * TRI_C]).astype(jnp.bfloat16).reshape(AMINO_SITES, AMINO_SITES, TRI_C)
    tri_right = (jax.nn.sigmoid(tri_projected[:, 2 * TRI_C:3 * TRI_C]) * tri_projected[:, 3 * TRI_C:]).astype(jnp.bfloat16).reshape(AMINO_SITES, AMINO_SITES, TRI_C)
    tri_sum = jnp.einsum('kic,kjc->ijc', tri_left.astype(jnp.float32), tri_right.astype(jnp.float32), precision=lax.Precision.HIGHEST).astype(jnp.bfloat16)
    tri_normed = layer_normalize(tri_sum.astype(jnp.float32)).astype(jnp.bfloat16).reshape(AMINO_SITES * AMINO_SITES, TRI_C)
    tri_gating = jax.nn.sigmoid(jnp.dot(pair_flat, triangle_output_gate, preferred_element_type=jnp.float32))
    pair_state_output = updated.astype(jnp.float32).reshape(AMINO_SITES * AMINO_SITES, CZ) + tri_gating * jnp.dot(tri_normed, triangle_output_weight, preferred_element_type=jnp.float32)
    pair_state_output = pair_state_output.astype(jnp.bfloat16).reshape(AMINO_SITES, AMINO_SITES, CZ)
    scorer_mapped_lines = jnp.dot(homolog_lines_merged, scorer_entry_coefficients, preferred_element_type=jnp.float32)
    asking_vectors = scorer_mapped_lines[:, :HOMOLOG_FEATS].astype(jnp.bfloat16).reshape(HOMOLOG_LINES, AMINO_SITES, SCORER_GROUPS, SCORER_SPAN)
    lookup_lines = scorer_mapped_lines[:, HOMOLOG_FEATS:2 * HOMOLOG_FEATS].astype(jnp.bfloat16).reshape(HOMOLOG_LINES, AMINO_SITES, SCORER_GROUPS, SCORER_SPAN)
    content_lines = scorer_mapped_lines[:, 2 * HOMOLOG_FEATS:3 * HOMOLOG_FEATS].astype(jnp.bfloat16).reshape(HOMOLOG_LINES, AMINO_SITES, SCORER_GROUPS, SCORER_SPAN)
    sigmoid_factor = scorer_mapped_lines[:, 3 * HOMOLOG_FEATS:].astype(jnp.bfloat16).reshape(HOMOLOG_LINES, AMINO_SITES, SCORER_GROUPS, SCORER_SPAN)
    mask_term = 1000000000.0 * (active_entry_mask - 1.0)
    bias_wide = head_bias.astype(jnp.float32)
    score_scale = SCORER_SPAN ** (-0.5)

    def attend(row_inputs):
        query_row, key_row, value_row, gate_row, mask_row = row_inputs
        scores = jnp.einsum('ihd,jhd->hij', query_row.astype(jnp.float32), key_row.astype(jnp.float32), precision=lax.Precision.HIGHEST) * score_scale
        scores = scores + bias_wide + mask_row[None, None, :]
        weights = jax.nn.softmax(scores, axis=-1).astype(jnp.bfloat16)
        attended = jnp.einsum('hij,jhd->ihd', weights.astype(jnp.float32), value_row.astype(jnp.float32), precision=lax.Precision.HIGHEST)
        return (jax.nn.sigmoid(gate_row.astype(jnp.float32)) * attended).astype(jnp.bfloat16)
    sigmoid_scaled_lines = lax.map(attend, (asking_vectors, lookup_lines, content_lines, sigmoid_factor, mask_term))
    homolog_revised = homolog_matrix.astype(jnp.float32).reshape(HOMOLOG_LINES * AMINO_SITES, HOMOLOG_FEATS) + jnp.dot(sigmoid_scaled_lines.reshape(HOMOLOG_LINES * AMINO_SITES, HOMOLOG_FEATS), scorer_final_coefficients, preferred_element_type=jnp.float32)
    homolog_revised = homolog_revised.astype(jnp.bfloat16).reshape(HOMOLOG_LINES, AMINO_SITES, HOMOLOG_FEATS)
    return (homolog_revised, pair_state_output)
```

```python
import functools
import jax
import jax.numpy as jnp
from jax import lax
from jax.experimental import pallas as pl
from jax.experimental.pallas import tpu as pltpu
from jax.sharding import PartitionSpec as P

REL_MAX = 32
F32 = jnp.float32
BF16 = jnp.bfloat16
OVER_FIRST = (((0,), (0,)), ((), ()))
OVER_LAST = (((1,), (1,)), ((), ()))


def mm(a, b):
    return jnp.dot(a, b, preferred_element_type=F32)


def norm_over(values, axis):
    centre = jnp.mean(values, axis=axis, keepdims=True)
    shifted = values - centre
    spread = jnp.mean(shifted * shifted, axis=axis, keepdims=True)
    return shifted * lax.rsqrt(spread + 1e-05)


def fused(
    n, msa, live_in, pair, chain, number, table, w_factor, w_outer, w_entry, w_final, w_bias, w_tri, w_gate, w_out,
    msa_out, pair_out,
    left_send, left_recv, right_send, right_recv, tri_send, tri_recv, bias_send, bias_recv, sum_send, sum_recv,
    wide, outer_cat, w_outer_t, w_tri_t, base, qkvg, count, bias_wide,
    send_sem, recv_sem,
):
    me = lax.axis_index("row")
    rows, res, feats = msa.shape
    own, _, cz = pair.shape
    fac = w_factor.shape[1] // 2
    heads = w_bias.shape[1]
    span = feats // heads
    tri = w_out.shape[0]
    per = tri // n
    chunk = right_send.shape[0]

    barrier = pltpu.get_barrier_semaphore()

    def greet(t, _):
        pl.semaphore_signal(
            barrier, inc=1, device_id={"row": lax.rem(me + t, n)}, device_id_type=pl.DeviceIdType.MESH
        )
        return 0

    lax.fori_loop(1, n, greet, 0)

    def copy_to(phase, t, src, dst):
        return pltpu.make_async_remote_copy(
            src_ref=src,
            dst_ref=dst,
            send_sem=send_sem.at[phase, t],
            recv_sem=recv_sem.at[phase, me],
            device_id={"row": lax.rem(me + t, n)},
            device_id_type=pl.DeviceIdType.MESH,
        )

    def arrived(phase, t, src, dst):
        return pltpu.make_async_remote_copy(
            src_ref=src,
            dst_ref=dst,
            send_sem=send_sem.at[phase, t],
            recv_sem=recv_sem.at[phase, lax.rem(me + t, n)],
            device_id={"row": lax.rem(me + t, n)},
            device_id_type=pl.DeviceIdType.MESH,
        )

    live = live_in[...].astype(F32)
    factor_t = jnp.concatenate(
        [jnp.transpose(w_factor[...].astype(F32)), jnp.zeros((2 * fac, feats), F32)], axis=0
    ).astype(BF16)
    normed = []
    for s in range(rows):
        normed.append(norm_over(msa[s].astype(F32), 1).astype(BF16))
        factors = lax.dot_general(factor_t, normed[s], OVER_LAST, preferred_element_type=F32)
        factors = factors * live[s : s + 1, :]
        right_send[s * fac : (s + 1) * fac, :] = factors[fac : 2 * fac].astype(BF16)
        wide[pl.ds(s, res, stride=rows), :] = jnp.transpose(factors)
    right_send[rows * fac :, :] = jnp.concatenate(
        [live, jnp.zeros((chunk - rows * fac - rows, res), F32)], axis=0
    ).astype(BF16)
    left_send[...] = wide[0 : res * rows, :].reshape(left_send.shape)

    pl.semaphore_wait(barrier, n - 1)

    def send_factors(t, _):
        to = lax.rem(me + t, n)
        copy_to(0, t, right_send, right_recv.at[me]).start()
        copy_to(1, t, left_send.at[to], left_recv.at[me]).start()
        return 0

    lax.fori_loop(1, n, send_factors, 0)
    right_recv[me] = right_send[...]
    left_recv[me] = left_send[me]

    wide[0 : fac * fac, :] = w_outer[...].astype(F32)
    for e in range(fac):
        outer_cat[e * fac : (e + 1) * fac, 0:cz] = wide[pl.ds(e, fac, stride=fac), :].astype(BF16)
    w_outer_t[...] = jnp.transpose(outer_cat[:, 0:cz].astype(F32)).astype(BF16)
    for b in range(4):
        w_tri_t[b * tri : (b + 1) * tri, :] = jnp.transpose(
            w_tri[:, b * tri : (b + 1) * tri].astype(F32)
        ).astype(BF16)
    gate_t = jnp.transpose(w_gate[...].astype(F32)).astype(BF16)
    out_t = jnp.transpose(w_out[...].astype(F32)).astype(BF16)
    for s in range(rows):
        qkvg[s] = mm(normed[s], w_entry[...]).astype(BF16)
    lane = lax.broadcasted_iota(jnp.int32, (1, res), 1)
    bins = table.shape[0]
    padded = table.shape[0] + (-table.shape[0]) % 8
    slot = lax.broadcasted_iota(jnp.int32, (bins, res), 0).astype(F32)
    chain_row = chain[...].astype(F32)
    number_row = number[...].astype(F32)
    for i in range(own):
        mine = lane == me * own + i
        chain_i = jnp.sum(jnp.where(mine, chain_row, 0.0), axis=1, keepdims=True)
        number_i = jnp.sum(jnp.where(mine, number_row, 0.0), axis=1, keepdims=True)
        offset = jnp.clip(number_i - number_row, -float(REL_MAX), float(REL_MAX)) + float(REL_MAX)
        kind = jnp.where(chain_i == chain_row, offset, float(2 * REL_MAX + 1))
        hot = jnp.where(slot == kind, 1.0, 0.0)
        term = lax.dot_general(
            table[...], hot, OVER_FIRST, precision=lax.Precision.HIGHEST, preferred_element_type=F32
        )
        base[:, i * res : (i + 1) * res] = jnp.transpose(pair[i].astype(F32)) + term

    def wait_factors(t, _):
        frm = lax.rem(me + t, n)
        arrived(0, t, right_send, right_recv.at[frm]).wait()
        arrived(1, t, left_send.at[frm], left_recv.at[frm]).wait()
        return 0

    lax.fori_loop(1, n, wait_factors, 0)

    left_flat = left_recv.reshape(n * own * rows, cz)
    left_rows = []
    for i in range(own):
        part = jnp.concatenate(
            [left_flat[pl.ds(i * rows + s, n, stride=own * rows), :] for s in range(rows)], axis=0
        )
        left_rows.append(jnp.transpose(part)[0:fac])
    left_t = jnp.concatenate(left_rows, axis=0).astype(BF16)
    wide[0 : n * chunk, :] = right_recv[...].astype(F32).reshape(n * chunk, res)

    def right_at(k):
        return jnp.concatenate(
            [wide[pl.ds(s * fac + k, n, stride=chunk), :] for s in range(rows)], axis=0
        ).astype(BF16)

    live_all = jnp.concatenate(
        [wide[pl.ds(rows * fac + s, n, stride=chunk), :] for s in range(rows)], axis=0
    )
    count[...] = mm(jnp.transpose(live_all).astype(BF16), live_all.astype(BF16))
    for e in range(fac):
        product = mm(left_t, right_at(e)).astype(BF16)
        for i in range(own):
            outer_cat[e * fac : (e + 1) * fac, i * res : (i + 1) * res] = product[i * fac : (i + 1) * fac]
    opm = mm(w_outer_t[...], outer_cat[...])
    for i in range(own):
        cols = slice(i * res, (i + 1) * res)
        base[:, cols] = base[:, cols] + opm[:, cols] / (0.001 + count[pl.ds(me * own + i, 1), :])
    updated = base[...].astype(BF16).astype(F32)
    base[...] = updated
    pair_norm = norm_over(updated, 0).astype(BF16)

    projected = mm(w_tri_t[...], pair_norm)
    both = (
        jax.nn.sigmoid(projected[0:tri]) * projected[tri : 2 * tri],
        jax.nn.sigmoid(projected[2 * tri : 3 * tri]) * projected[3 * tri :],
    )
    lines = 2 * per * own
    for side in range(2):
        for c in range(per):
            for k in range(own):
                wide[pl.ds((side * per + c) * own + k, n, stride=lines), :] = both[side][
                    c * n : (c + 1) * n, k * res : (k + 1) * res
                ]
    tri_send[...] = wide[0 : n * lines, :].astype(BF16).reshape(tri_send.shape)
    bias_t = lax.dot_general(w_bias[...], pair_norm, OVER_FIRST, preferred_element_type=F32)
    bias_send[...] = jnp.concatenate(
        [bias_t[:, i * res : (i + 1) * res] for i in range(own)], axis=0
    ).astype(BF16)

    def send_tri(t, _):
        to = lax.rem(me + t, n)
        copy_to(2, t, tri_send.at[to], tri_recv.at[me]).start()
        return 0

    def send_bias(t, _):
        copy_to(3, t, bias_send, bias_recv.at[me]).start()
        return 0

    lax.fori_loop(1, n, send_tri, 0)
    lax.fori_loop(1, n, send_bias, 0)
    tri_recv[me] = tri_send[me]
    bias_recv[me] = bias_send[...]
    gating = jax.nn.sigmoid(mm(gate_t, pair_norm))

    def wait_tri(t, _):
        frm = lax.rem(me + t, n)
        arrived(2, t, tri_send.at[frm], tri_recv.at[frm]).wait()
        return 0

    lax.fori_loop(1, n, wait_tri, 0)
    wide[0 : n * lines, :] = tri_recv[...].astype(F32).reshape(n * lines, res)
    sums = []
    for c in range(per):
        left_c, right_c = (
            jnp.concatenate(
                [wide[pl.ds((side * per + c) * own + k, n, stride=lines), :] for k in range(own)], axis=0
            )
            for side in range(2)
        )
        sums.append(mm(jnp.transpose(left_c).astype(BF16), right_c.astype(BF16)))
    for c in range(per):
        wide[pl.ds(c, res, stride=per), :] = sums[c]
    sum_send[...] = wide[0 : res * per, :].astype(BF16).reshape(sum_send.shape)

    def send_sum(t, _):
        to = lax.rem(me + t, n)
        copy_to(4, t, sum_send.at[to], sum_recv.at[me]).start()
        return 0

    lax.fori_loop(1, n, send_sum, 0)
    sum_recv[me] = sum_send[me]

    def wait_bias(t, _):
        frm = lax.rem(me + t, n)
        arrived(3, t, bias_send, bias_recv.at[frm]).wait()
        return 0

    lax.fori_loop(1, n, wait_bias, 0)
    bias_wide[...] = bias_recv[...].astype(F32).reshape(bias_wide.shape)
    column = lax.broadcasted_iota(jnp.int32, (1, feats), 1)
    scale = span ** (-0.5)
    for s in range(rows):
        query = qkvg[s, :, 0:feats]
        key = qkvg[s, :, feats : 2 * feats]
        value = qkvg[s, :, 2 * feats : 3 * feats]
        gate = jax.nn.sigmoid(qkvg[s, :, 3 * feats :].astype(F32))
        mask = 1000000000.0 * (live[s : s + 1, :] - 1.0)
        attended = jnp.zeros((res, feats), F32)
        for h in range(heads):
            at_head = (column >= h * span) & (column < (h + 1) * span)
            scores = lax.dot_general(
                jnp.where(at_head, query, jnp.zeros_like(query)), key, OVER_LAST, preferred_element_type=F32
            )
            scores = scores * scale + bias_wide[pl.ds(h, res, stride=heads), :] + mask
            scores = jnp.exp(scores - jnp.max(scores, axis=1, keepdims=True))
            weights = (scores / jnp.sum(scores, axis=1, keepdims=True)).astype(BF16)
            attended = jnp.where(at_head, mm(weights, value), attended)
        gated = (gate * attended).astype(BF16)
        msa_out[s] = (msa[s].astype(F32) + mm(gated, w_final[...])).astype(BF16)

    def wait_sum(t, _):
        frm = lax.rem(me + t, n)
        arrived(4, t, sum_send.at[frm], sum_recv.at[frm]).wait()
        return 0

    lax.fori_loop(1, n, wait_sum, 0)
    wide[0 : res * per, :] = sum_recv[...].astype(F32).reshape(res * per, res)
    for i in range(own):
        tri_sum = jnp.concatenate(
            [wide[pl.ds(i * per + c, n, stride=own * per), :] for c in range(per)], axis=0
        )
        tri_normed = norm_over(tri_sum, 0).astype(BF16)
        cols = slice(i * res, (i + 1) * res)
        result = base[:, cols] + gating[:, cols] * mm(out_t, tri_normed)
        pair_out[i] = jnp.transpose(result).astype(BF16)


def fused_on_device(
    n, msa, live, pair, chain, number, table, w_factor, w_outer, w_entry, w_final, w_bias, w_tri, w_gate, w_out
):
    rows, res, feats = msa.shape
    own, _, cz = pair.shape
    fac = w_factor.shape[1] // 2
    heads = w_bias.shape[1]
    tri = w_out.shape[0]
    per = tri // n
    chunk = rows * fac + 16
    lines = 2 * per * own
    wide_rows = max(n * chunk, n * lines, fac * fac, rows * res, per * res)
    vmem = pl.BlockSpec(memory_space=pltpu.VMEM)
    return pl.pallas_call(
        functools.partial(fused, n),
        out_shape=(jax.ShapeDtypeStruct(msa.shape, BF16), jax.ShapeDtypeStruct(pair.shape, BF16)),
        in_specs=[vmem] * 14,
        out_specs=(vmem, vmem),
        scratch_shapes=[
            pltpu.VMEM((n, own * rows, res), F32),
            pltpu.VMEM((n, own * rows, res), F32),
            pltpu.VMEM((chunk, res), BF16),
            pltpu.VMEM((n, chunk, res), BF16),
            pltpu.VMEM((n, lines, res), BF16),
            pltpu.VMEM((n, lines, res), BF16),
            pltpu.VMEM((own * heads, res), BF16),
            pltpu.VMEM((n, own * heads, res), BF16),
            pltpu.VMEM((n, own * per, res), BF16),
            pltpu.VMEM((n, own * per, res), BF16),
            pltpu.VMEM((wide_rows, res), F32),
            pltpu.VMEM((fac * fac, own * res), BF16),
            pltpu.VMEM((cz, fac * fac), BF16),
            pltpu.VMEM((4 * tri, cz), BF16),
            pltpu.VMEM((cz, own * res), F32),
            pltpu.VMEM((rows, res, 4 * feats), BF16),
            pltpu.VMEM((res, res), F32),
            pltpu.VMEM((n * own * heads, res), F32),
            pltpu.SemaphoreType.DMA((5, n)),
            pltpu.SemaphoreType.DMA((5, n)),
        ],
        compiler_params=pltpu.CompilerParams(
            collective_id=0, has_side_effects=True, vmem_limit_bytes=48 * 1024 * 1024
        ),
    )(
        msa, live, pair, chain.reshape(1, res), number.reshape(1, res), table,
        w_factor, w_outer, w_entry, w_final, w_bias, w_tri, w_gate, w_out,
    )


def layer_normalize(values):
    centre = jnp.mean(values, axis=-1, keepdims=True)
    shifted = values - centre
    spread = jnp.mean(shifted * shifted, axis=-1, keepdims=True)
    return shifted * lax.rsqrt(spread + 1e-05)


def on_device(
    homolog_matrix,
    alignment_mask,
    pair_state_input,
    chain_label,
    residue_number_index,
    relative_position_table,
    tensor_factor_coefficients,
    outer_output_weight,
    scorer_entry_coefficients,
    scorer_final_coefficients,
    pair_bias_weight,
    triangle_input_weight,
    triangle_output_gate,
    triangle_output_weight,
):
    sequence_local_rows = homolog_matrix.shape[0]
    residue_total = homolog_matrix.shape[1]
    alignment_width = homolog_matrix.shape[2]
    res_local = pair_state_input.shape[0]
    pair_width = pair_state_input.shape[2]
    opm_width = tensor_factor_coefficients.shape[1] // 2
    head_total = pair_bias_weight.shape[1]
    head_channel_width = alignment_width // head_total
    tri_width = triangle_input_weight.shape[1] // 4
    table_rows = relative_position_table.shape[0]
    row_start = lax.axis_index("row") * res_local
    contract = (((0,), (0,)), ((), ()))
    active_entry_mask = alignment_mask.astype(jnp.float32)
    homolog_rescaled = layer_normalize(homolog_matrix.astype(jnp.float32)).astype(jnp.bfloat16)
    homolog_lines_merged = homolog_rescaled.reshape(
        sequence_local_rows * residue_total, alignment_width
    )
    projected_rows = jnp.dot(
        homolog_lines_merged, tensor_factor_coefficients, preferred_element_type=jnp.float32
    ).reshape(sequence_local_rows, residue_total, 2 * opm_width)
    left_factor = (
        (projected_rows[..., :opm_width] * active_entry_mask[..., None])
        .astype(jnp.bfloat16)
        .reshape(sequence_local_rows, residue_total * opm_width)
    )
    right_factor = (
        (projected_rows[..., opm_width:] * active_entry_mask[..., None])
        .astype(jnp.bfloat16)
        .reshape(sequence_local_rows, residue_total * opm_width)
    )
    live_weights = active_entry_mask.astype(jnp.bfloat16)
    left_all, right_all, live_all = (
        lax.all_gather(left_factor, "row", axis=0, tiled=True),
        lax.all_gather(right_factor, "row", axis=0, tiled=True),
        lax.all_gather(live_weights, "row", axis=0, tiled=True),
    )
    left_cols = lax.dynamic_slice_in_dim(left_all, row_start * opm_width, res_local * opm_width, 1)
    live_cols = lax.dynamic_slice_in_dim(live_all, row_start, res_local, 1)
    outer_sum = lax.dot_general(left_cols, right_all, contract, preferred_element_type=jnp.float32)
    pair_count = lax.dot_general(live_cols, live_all, contract, preferred_element_type=jnp.float32)
    outer_flat = outer_sum.reshape(res_local, opm_width, residue_total, opm_width).transpose(
        0, 2, 1, 3
    )
    outer_flat = outer_flat.reshape(res_local * residue_total, opm_width * opm_width).astype(
        jnp.bfloat16
    )
    opm_update = jnp.dot(
        outer_flat, outer_output_weight, preferred_element_type=jnp.float32
    ).reshape(res_local, residue_total, pair_width)
    opm_update = opm_update / (0.001 + pair_count[..., None])
    chain_rows = lax.dynamic_slice_in_dim(chain_label, row_start, res_local, 0)
    index_rows = lax.dynamic_slice_in_dim(residue_number_index, row_start, res_local, 0)
    same_chain = chain_rows[:, None] == chain_label[None, :]
    offsets = (
        jnp.clip(index_rows[:, None] - residue_number_index[None, :], -REL_MAX, REL_MAX) + REL_MAX
    )
    bin_index = jnp.where(same_chain, offsets, 2 * REL_MAX + 1)
    one_hot = (
        (bin_index[..., None] == jnp.arange(table_rows, dtype=jnp.int32))
        .astype(jnp.float32)
        .reshape(-1, table_rows)
    )
    position_term = jnp.dot(
        one_hot, relative_position_table, precision=lax.Precision.HIGHEST
    ).reshape(res_local, residue_total, pair_width)
    updated = (pair_state_input.astype(jnp.float32) + position_term + opm_update).astype(
        jnp.bfloat16
    )
    pair_norm = layer_normalize(updated.astype(jnp.float32)).astype(jnp.bfloat16)
    pair_flat = pair_norm.reshape(res_local * residue_total, pair_width)
    head_bias = jnp.dot(pair_flat, pair_bias_weight, preferred_element_type=jnp.float32).astype(
        jnp.bfloat16
    )
    head_bias = head_bias.reshape(res_local, residue_total, head_total).transpose(2, 0, 1)
    full_bias = lax.all_gather(head_bias, "row", axis=1, tiled=True)
    tri_projected = jnp.dot(pair_flat, triangle_input_weight, preferred_element_type=jnp.float32)
    tri_left = (
        jax.nn.sigmoid(tri_projected[:, :tri_width]) * tri_projected[:, tri_width : 2 * tri_width]
    ).astype(jnp.bfloat16)
    tri_right = (
        jax.nn.sigmoid(tri_projected[:, 2 * tri_width : 3 * tri_width])
        * tri_projected[:, 3 * tri_width :]
    ).astype(jnp.bfloat16)
    tri_left = tri_left.reshape(res_local, residue_total, tri_width).transpose(2, 0, 1)
    tri_right = tri_right.reshape(res_local, residue_total, tri_width).transpose(2, 0, 1)
    left_channels, right_channels = (
        lax.all_to_all(tri_left, "row", split_axis=0, concat_axis=1, tiled=True),
        lax.all_to_all(tri_right, "row", split_axis=0, concat_axis=1, tiled=True),
    )
    channel_sum = jnp.einsum(
        "cki,ckj->cij", left_channels, right_channels, preferred_element_type=jnp.float32
    ).astype(jnp.bfloat16)
    row_sum = lax.all_to_all(channel_sum, "row", split_axis=1, concat_axis=0, tiled=True)
    tri_sum = row_sum.transpose(1, 2, 0)
    tri_normed = (
        layer_normalize(tri_sum.astype(jnp.float32))
        .astype(jnp.bfloat16)
        .reshape(res_local * residue_total, tri_width)
    )
    tri_gating = jax.nn.sigmoid(
        jnp.dot(pair_flat, triangle_output_gate, preferred_element_type=jnp.float32)
    )
    pair_state_output = updated.astype(jnp.float32).reshape(
        res_local * residue_total, pair_width
    ) + tri_gating * jnp.dot(tri_normed, triangle_output_weight, preferred_element_type=jnp.float32)
    pair_state_output = pair_state_output.astype(jnp.bfloat16).reshape(
        res_local, residue_total, pair_width
    )
    scorer_mapped_lines = jnp.dot(
        homolog_lines_merged, scorer_entry_coefficients, preferred_element_type=jnp.float32
    )
    asking_vectors = (
        scorer_mapped_lines[:, :alignment_width]
        .astype(jnp.bfloat16)
        .reshape(sequence_local_rows, residue_total, head_total, head_channel_width)
    )
    lookup_lines = (
        scorer_mapped_lines[:, alignment_width : 2 * alignment_width]
        .astype(jnp.bfloat16)
        .reshape(sequence_local_rows, residue_total, head_total, head_channel_width)
    )
    content_lines = (
        scorer_mapped_lines[:, 2 * alignment_width : 3 * alignment_width]
        .astype(jnp.bfloat16)
        .reshape(sequence_local_rows, residue_total, head_total, head_channel_width)
    )
    sigmoid_factor = (
        scorer_mapped_lines[:, 3 * alignment_width :]
        .astype(jnp.bfloat16)
        .reshape(sequence_local_rows, residue_total, head_total, head_channel_width)
    )
    mask_term = 1000000000.0 * (active_entry_mask - 1.0)
    score_scale = head_channel_width ** (-0.5)

    def attend(row_inputs):
        query_row, key_row, value_row, gate_row, mask_row = row_inputs
        scores = (
            jnp.einsum("ihd,jhd->hij", query_row, key_row, preferred_element_type=jnp.float32)
            * score_scale
        )
        scores = scores + full_bias.astype(jnp.float32) + mask_row[None, None, :]
        weights = jax.nn.softmax(scores, axis=-1).astype(jnp.bfloat16)
        attended = jnp.einsum(
            "hij,jhd->ihd", weights, value_row, preferred_element_type=jnp.float32
        )
        return (jax.nn.sigmoid(gate_row.astype(jnp.float32)) * attended).astype(jnp.bfloat16)

    sigmoid_scaled_lines = lax.map(
        attend, (asking_vectors, lookup_lines, content_lines, sigmoid_factor, mask_term)
    )
    homolog_revised = homolog_matrix.astype(jnp.float32).reshape(
        sequence_local_rows * residue_total, alignment_width
    ) + jnp.dot(
        sigmoid_scaled_lines.reshape(sequence_local_rows * residue_total, alignment_width),
        scorer_final_coefficients,
        preferred_element_type=jnp.float32,
    )
    homolog_revised = homolog_revised.astype(jnp.bfloat16).reshape(
        sequence_local_rows, residue_total, alignment_width
    )
    return (homolog_revised, pair_state_output)


def solution(mesh):
    n = mesh.shape["row"]

    def body(*blocks):
        msa, pair, w_out = blocks[0], blocks[2], blocks[13]
        rows, res, _ = msa.shape
        fits = (
            res == pair.shape[2] == w_out.shape[0] == 128
            and res % n == 0
            and w_out.shape[0] % n == 0
            and (res // n) * rows == 8
        )
        return fused_on_device(n, *blocks) if fits else on_device(*blocks)

    return jax.shard_map(
        body,
        mesh=mesh,
        in_specs=(
            P(("grp", "row"), None, None),
            P(("grp", "row"), None),
            P(("grp", "row"), None, None),
            P("grp"),
            P("grp"),
            P(),
            P(),
            P(),
            P(),
            P(),
            P(),
            P(),
            P(),
            P(),
        ),
        out_specs=(P(("grp", "row"), None, None), P(("grp", "row"), None, None)),
        check_vma=False,
    )
```

```python
import functools
import jax
import jax.numpy as jnp
from jax import lax
from jax.experimental import pallas as pl
from jax.experimental.pallas import tpu as pltpu
from jax.sharding import PartitionSpec as P

REL_MAX = 32
F32 = jnp.float32
BF16 = jnp.bfloat16
LEFT = jnp.bfloat16
OVER_FIRST = (((0,), (0,)), ((), ()))
OVER_LAST = (((1,), (1,)), ((), ()))


def mm(a, b):
    return jnp.dot(a, b, preferred_element_type=F32)


def norm_over(values, axis):
    centre = jnp.mean(values, axis=axis, keepdims=True)
    shifted = values - centre
    spread = jnp.mean(shifted * shifted, axis=axis, keepdims=True)
    return shifted * lax.rsqrt(spread + 1e-05)


def fused(
    n, *refs
):
    inputs, (msa_out, pair_out), landed = refs[:14], refs[14:16], refs[16:30]
    fused_body(n, inputs, landed, msa_out, pair_out, *refs[30:])


def fused_body(
    n, inputs, landed, msa_out, pair_out,
    left_send, left_recv, right_send, right_recv, tri_send, tri_recv, bias_send, bias_recv, sum_send, sum_recv,
    wide, outer_cat, w_outer_t, w_tri_t, base, qkvg, count, bias_wide, outer_wide,
    send_sem, recv_sem, load_sem,
):
    msa, live_in, pair, chain, number, table, w_factor, w_outer, w_entry, w_final, w_bias, w_tri, w_gate, w_out = landed
    me = lax.axis_index("row")
    core = lax.rem(me, 2)
    chip = me // 2
    chips = n // 2
    sibling = me + 1 - 2 * core
    loads = [pltpu.make_async_copy(inputs[k], landed[k], load_sem.at[k]) for k in range(14)]
    for k in (0, 1, 6, 7, 8, 2, 11, 3, 4, 5, 12, 13, 9, 10):
        loads[k].start()
    rows, res, feats = msa.shape
    own, _, cz = pair.shape
    fac = w_factor.shape[0] // 2
    heads = w_bias.shape[0]
    span = feats // heads
    tri = w_out.shape[0]
    per = tri // n
    chunk = right_send.shape[0]

    barrier = pltpu.get_barrier_semaphore()

    def greet(t, _):
        pl.semaphore_signal(
            barrier, inc=1, device_id={"row": lax.rem(me + t, n)}, device_id_type=pl.DeviceIdType.MESH
        )
        return 0

    lax.fori_loop(1, n, greet, 0)

    def copy_to(phase, t, src, dst):
        return pltpu.make_async_remote_copy(
            src_ref=src,
            dst_ref=dst,
            send_sem=send_sem.at[phase, t],
            recv_sem=recv_sem.at[phase, me],
            device_id={"row": lax.rem(me + t, n)},
            device_id_type=pl.DeviceIdType.MESH,
        )

    def arrived(phase, t, src, dst):
        return pltpu.make_async_remote_copy(
            src_ref=src,
            dst_ref=dst,
            send_sem=send_sem.at[phase, t],
            recv_sem=recv_sem.at[phase, lax.rem(me + t, n)],
            device_id={"row": lax.rem(me + t, n)},
            device_id_type=pl.DeviceIdType.MESH,
        )

    for k in (0, 1, 6):
        loads[k].wait()
    live = live_in[...].astype(F32)
    factor_t = jnp.concatenate(
        [w_factor[...].astype(F32), jnp.zeros((2 * fac, feats), F32)], axis=0
    ).astype(BF16)
    normed = []
    base_row = n * chunk
    wide[base_row : base_row + 8 * n, :] = jnp.zeros((8 * n, res), F32)
    for s in range(rows):
        normed.append(norm_over(msa[s].astype(F32), 1).astype(BF16))
        factors = lax.dot_general(factor_t, normed[s], OVER_LAST, preferred_element_type=F32)
        factors = factors * live[s : s + 1, :]
        right_send[s * fac : (s + 1) * fac, :] = factors[fac : 2 * fac].astype(BF16)
        count[...] = jnp.transpose(
            jnp.concatenate([factors[0:fac], jnp.zeros((res - fac, res), F32)], axis=0)
        )
        packed = count[pl.ds(0, n, stride=own), :]
        for i in range(1, own):
            packed = packed + pltpu.roll(count[pl.ds(i, n, stride=own), :], i * fac, 1)
        wide[pl.ds(base_row + s, n, stride=8), :] = packed
        wide[pl.ds(base_row + rows + s, n, stride=8), :] = jnp.broadcast_to(live[s : s + 1, :], (n, res))
    left_send[...] = wide[base_row : base_row + 8 * n, :].astype(left_send.dtype).reshape(left_send.shape)

    pl.semaphore_wait(barrier, n - 1)

    def to_device(src, dst, out_sem, in_sem, device):
        return pltpu.make_async_remote_copy(
            src_ref=src, dst_ref=dst, send_sem=out_sem, recv_sem=in_sem,
            device_id={"row": device}, device_id_type=pl.DeviceIdType.MESH,
        )

    def right_out(t):
        to = lax.rem(chip + t, chips) * 2 + core
        return to_device(right_send, right_recv.at[me], send_sem.at[0, t], recv_sem.at[0, me], to)

    def right_on(t):
        frm = lax.rem(chip + chips - t, chips) * 2 + core
        return to_device(
            right_recv.at[frm], right_recv.at[frm], send_sem.at[0, chips + t], recv_sem.at[0, frm], sibling
        )

    def right_in(frm):
        return to_device(right_send, right_recv.at[frm], send_sem.at[0, 0], recv_sem.at[0, frm], sibling)

    def send_right(t, _):
        right_out(t).start()
        return 0

    def send_left(t, _):
        to = lax.rem(me + t, n)
        copy_to(1, t, left_send.at[to], left_recv.at[me]).start()
        return 0

    def widen_right(frm):
        wide[pl.ds(pl.multiple_of(frm * chunk, chunk), chunk), :] = right_recv[frm].astype(F32)

    def hand_on(t, _):
        frm = lax.rem(chip + chips - t, chips) * 2 + core
        right_in(frm).wait_recv()
        right_on(t).start()
        widen_right(frm)
        return 0

    lax.fori_loop(1, chips, send_right, 0)
    to_sibling = to_device(right_send, right_recv.at[me], send_sem.at[0, 0], recv_sem.at[0, me], sibling)
    to_sibling.start()
    lax.fori_loop(1, n, send_left, 0)
    right_recv[me] = right_send[...]
    widen_right(me)
    left_recv[me] = left_send[me]

    loads[7].wait()
    outer_wide[...] = w_outer[...].astype(F32)
    for e in range(fac):
        outer_cat[e * fac : (e + 1) * fac, 0:cz] = outer_wide[pl.ds(e, fac, stride=fac), :].astype(BF16)
    w_outer_t[...] = jnp.transpose(outer_cat[:, 0:cz].astype(F32)).astype(BF16)
    lax.fori_loop(1, 1 + chips // 4, hand_on, 0)
    for k in (8, 11, 12, 13):
        loads[k].wait()
    for b in range(4):
        w_tri_t[b * tri : (b + 1) * tri, :] = jnp.transpose(
            w_tri[:, b * tri : (b + 1) * tri].astype(F32)
        ).astype(BF16)
    gate_t = jnp.transpose(w_gate[...].astype(F32)).astype(BF16)
    out_t = jnp.transpose(w_out[...].astype(F32)).astype(BF16)
    for s in range(rows):
        qkvg[s] = mm(normed[s], w_entry[...]).astype(BF16)
    lax.fori_loop(1 + chips // 4, 1 + chips // 2, hand_on, 0)
    for k in (2, 3, 4, 5):
        loads[k].wait()
    lane = lax.broadcasted_iota(jnp.int32, (1, res), 1)
    bins = table.shape[0]
    padded = table.shape[0] + (-table.shape[0]) % 8
    slot = lax.broadcasted_iota(jnp.int32, (bins, res), 0).astype(F32)
    chain_row = chain[...].astype(F32)
    number_row = number[...].astype(F32)
    for i in range(own):
        mine = lane == me * own + i
        chain_i = jnp.sum(jnp.where(mine, chain_row, 0.0), axis=1, keepdims=True)
        number_i = jnp.sum(jnp.where(mine, number_row, 0.0), axis=1, keepdims=True)
        offset = jnp.clip(number_i - number_row, -float(REL_MAX), float(REL_MAX)) + float(REL_MAX)
        kind = jnp.where(chain_i == chain_row, offset, float(2 * REL_MAX + 1))
        hot = jnp.where(slot == kind, 1.0, 0.0)
        term = lax.dot_general(
            table[...], hot, OVER_FIRST, precision=lax.Precision.HIGHEST, preferred_element_type=F32
        )
        base[:, i * res : (i + 1) * res] = jnp.transpose(pair[i].astype(F32)) + term

    lax.fori_loop(1 + chips // 2, chips, hand_on, 0)

    def wait_left(t, _):
        frm = lax.rem(me + t, n)
        arrived(1, t, left_send.at[frm], left_recv.at[frm]).wait_recv()
        return 0

    def wait_sibling(t, _):
        frm = lax.rem(chip + chips - t, chips) * 2 + 1 - core
        right_in(frm).wait_recv()
        widen_right(frm)
        return 0

    lax.fori_loop(1, n, wait_left, 0)

    wide[base_row : base_row + 8 * n, :] = left_recv[...].astype(F32).reshape(8 * n, res)
    left_rows, live_rows = (
        jnp.concatenate([wide[pl.ds(base_row + r + s, n, stride=8), :] for s in range(rows)], axis=0)
        for r in (0, rows)
    )
    left_t = jnp.transpose(left_rows).astype(BF16)
    count[...] = mm(jnp.transpose(live_rows).astype(BF16), live_rows.astype(BF16))
    lax.fori_loop(0, chips, wait_sibling, 0)

    def right_at(k):
        return jnp.concatenate(
            [wide[pl.ds(s * fac + k, n, stride=chunk), :] for s in range(rows)], axis=0
        ).astype(BF16)

    for e in range(0, fac, 2):
        product = mm(left_t, jnp.concatenate([right_at(e), right_at(e + 1)], axis=1)).astype(BF16)
        for k in range(2):
            for i in range(own):
                outer_cat[(e + k) * fac : (e + k + 1) * fac, i * res : (i + 1) * res] = product[
                    i * fac : (i + 1) * fac, k * res : (k + 1) * res
                ]
    opm = mm(w_outer_t[...], outer_cat[...])
    for i in range(own):
        cols = slice(i * res, (i + 1) * res)
        base[:, cols] = base[:, cols] + opm[:, cols] * (1.0 / (0.001 + count[pl.ds(me * own + i, 1), :]))
    updated = base[...].astype(BF16).astype(F32)
    base[...] = updated
    pair_norm = norm_over(updated, 0).astype(BF16)

    projected = mm(w_tri_t[...], pair_norm)
    both = (
        jax.nn.sigmoid(projected[0:tri]) * projected[tri : 2 * tri],
        jax.nn.sigmoid(projected[2 * tri : 3 * tri]) * projected[3 * tri :],
    )
    lines = 2 * per * own
    for side in range(2):
        for c in range(per):
            for k in range(own):
                wide[pl.ds((side * per + c) * own + k, n, stride=lines), :] = both[side][
                    c * n : (c + 1) * n, k * res : (k + 1) * res
                ]
    tri_send[...] = wide[0 : n * lines, :].astype(BF16).reshape(tri_send.shape)
    def send_tri(t, _):
        to = lax.rem(me + t, n)
        copy_to(2, t, tri_send.at[to], tri_recv.at[me]).start()
        return 0

    def send_bias(t, _):
        copy_to(3, t, bias_send, bias_recv.at[me]).start()
        return 0

    lax.fori_loop(1, n, send_tri, 0)
    loads[10].wait()
    bias_t = mm(w_bias[...], pair_norm)
    bias_send[...] = jnp.concatenate(
        [bias_t[:, i * res : (i + 1) * res] for i in range(own)], axis=0
    ).astype(BF16)
    lax.fori_loop(1, n, send_bias, 0)
    tri_recv[me] = tri_send[me]
    bias_recv[me] = bias_send[...]
    gating = jax.nn.sigmoid(mm(gate_t, pair_norm))

    def wait_tri(t, _):
        frm = lax.rem(me + t, n)
        arrived(2, t, tri_send.at[frm], tri_recv.at[frm]).wait_recv()
        return 0

    lax.fori_loop(1, n, wait_tri, 0)
    wide[0 : n * lines, :] = tri_recv[...].astype(F32).reshape(n * lines, res)
    sums = []
    for c in range(per):
        left_c, right_c = (
            jnp.concatenate(
                [wide[pl.ds((side * per + c) * own + k, n, stride=lines), :] for k in range(own)], axis=0
            )
            for side in range(2)
        )
        sums.append(mm(jnp.transpose(left_c).astype(BF16), right_c.astype(BF16)))
    for c in range(per):
        wide[pl.ds(c, res, stride=per), :] = sums[c]
    sum_send[...] = wide[0 : res * per, :].astype(BF16).reshape(sum_send.shape)

    def send_sum(t, _):
        to = lax.rem(me + t, n)
        copy_to(4, t, sum_send.at[to], sum_recv.at[me]).start()
        return 0

    lax.fori_loop(1, n, send_sum, 0)
    sum_recv[me] = sum_send[me]

    loads[9].wait()
    def wait_bias(t, _):
        frm = lax.rem(me + t, n)
        arrived(3, t, bias_send, bias_recv.at[frm]).wait_recv()
        return 0

    lax.fori_loop(1, n, wait_bias, 0)
    bias_wide[...] = bias_recv[...].astype(F32).reshape(bias_wide.shape)
    column = lax.broadcasted_iota(jnp.int32, (1, feats), 1)
    scale = span ** (-0.5)
    for s in range(rows):
        query = qkvg[s, :, 0:feats]
        key = qkvg[s, :, feats : 2 * feats]
        value = qkvg[s, :, 2 * feats : 3 * feats]
        gate = jax.nn.sigmoid(qkvg[s, :, 3 * feats :].astype(F32))
        mask = 1000000000.0 * (live[s : s + 1, :] - 1.0)
        attended = jnp.zeros((res, feats), F32)
        for h in range(heads):
            at_head = (column >= h * span) & (column < (h + 1) * span)
            scores = lax.dot_general(
                jnp.where(at_head, query, jnp.zeros_like(query)), key, OVER_LAST, preferred_element_type=F32
            )
            scores = scores * scale + bias_wide[pl.ds(h, res, stride=heads), :] + mask
            scores = jnp.exp(scores - jnp.max(scores, axis=1, keepdims=True))
            weights = (scores * (1.0 / jnp.sum(scores, axis=1, keepdims=True))).astype(BF16)
            attended = jnp.where(at_head, mm(weights, value), attended)
        gated = (gate * attended).astype(BF16)
        msa_out[s] = (msa[s].astype(F32) + mm(gated, w_final[...])).astype(BF16)

    def wait_sum(t, _):
        frm = lax.rem(me + t, n)
        arrived(4, t, sum_send.at[frm], sum_recv.at[frm]).wait_recv()
        return 0

    lax.fori_loop(1, n, wait_sum, 0)
    wide[0 : res * per, :] = sum_recv[...].astype(F32).reshape(res * per, res)
    for i in range(own):
        tri_sum = jnp.concatenate(
            [wide[pl.ds(i * per + c, n, stride=own * per), :] for c in range(per)], axis=0
        )
        tri_normed = norm_over(tri_sum, 0).astype(BF16)
        cols = slice(i * res, (i + 1) * res)
        result = base[:, cols] + gating[:, cols] * mm(out_t, tri_normed)
        pair_out[i] = jnp.transpose(result).astype(BF16)

    def all_sent(t, _):
        to = lax.rem(me + t, n)
        copy_to(1, t, left_send.at[to], left_recv.at[me]).wait_send()
        copy_to(2, t, tri_send.at[to], tri_recv.at[me]).wait_send()
        copy_to(3, t, bias_send, bias_recv.at[me]).wait_send()
        copy_to(4, t, sum_send.at[to], sum_recv.at[me]).wait_send()
        return 0

    def right_sent(t, _):
        right_out(t).wait_send()
        right_on(t).wait_send()
        return 0

    lax.fori_loop(1, n, all_sent, 0)
    lax.fori_loop(1, chips, right_sent, 0)
    to_sibling.wait_send()


def fused_on_device(
    n, msa, live, pair, chain, number, table, w_factor, w_outer, w_entry, w_final, w_bias, w_tri, w_gate, w_out
):
    rows, res, feats = msa.shape
    own, _, cz = pair.shape
    fac = w_factor.shape[1] // 2
    heads = w_bias.shape[1]
    tri = w_out.shape[0]
    per = tri // n
    chunk = rows * fac
    lines = 2 * per * own
    wide_rows = max(n * chunk + 8 * n, n * lines, per * res)
    vmem = pl.BlockSpec(memory_space=pltpu.VMEM)
    args = (
        msa, live, pair, chain.reshape(1, res), number.reshape(1, res), table,
        w_factor.T, w_outer, w_entry, w_final, w_bias.T, w_tri, w_gate, w_out,
    )
    return pl.pallas_call(
        functools.partial(fused, n),
        out_shape=(jax.ShapeDtypeStruct(msa.shape, BF16), jax.ShapeDtypeStruct(pair.shape, BF16)),
        in_specs=[pl.BlockSpec(memory_space=pltpu.HBM)] * 14,
        out_specs=(vmem, vmem),
        scratch_shapes=[
            *[pltpu.VMEM(a.shape, a.dtype) for a in args],
            pltpu.VMEM((n, 8, res), LEFT),
            pltpu.VMEM((n, 8, res), LEFT),
            pltpu.VMEM((chunk, res), BF16),
            pltpu.VMEM((n, chunk, res), BF16),
            pltpu.VMEM((n, lines, res), BF16),
            pltpu.VMEM((n, lines, res), BF16),
            pltpu.VMEM((own * heads, res), BF16),
            pltpu.VMEM((n, own * heads, res), BF16),
            pltpu.VMEM((n, own * per, res), BF16),
            pltpu.VMEM((n, own * per, res), BF16),
            pltpu.VMEM((wide_rows, res), F32),
            pltpu.VMEM((fac * fac, own * res), BF16),
            pltpu.VMEM((cz, fac * fac), BF16),
            pltpu.VMEM((4 * tri, cz), BF16),
            pltpu.VMEM((cz, own * res), F32),
            pltpu.VMEM((rows, res, 4 * feats), BF16),
            pltpu.VMEM((res, res), F32),
            pltpu.VMEM((n * own * heads, res), F32),
            pltpu.VMEM((fac * fac, cz), F32),
            pltpu.SemaphoreType.DMA((5, n)),
            pltpu.SemaphoreType.DMA((5, n)),
            pltpu.SemaphoreType.DMA((14,)),
        ],
        compiler_params=pltpu.CompilerParams(
            collective_id=0, has_side_effects=True, vmem_limit_bytes=64 * 1024 * 1024 - 4096
        ),
    )(*args)


def layer_normalize(values):
    centre = jnp.mean(values, axis=-1, keepdims=True)
    shifted = values - centre
    spread = jnp.mean(shifted * shifted, axis=-1, keepdims=True)
    return shifted * lax.rsqrt(spread + 1e-05)


def on_device(
    homolog_matrix,
    alignment_mask,
    pair_state_input,
    chain_label,
    residue_number_index,
    relative_position_table,
    tensor_factor_coefficients,
    outer_output_weight,
    scorer_entry_coefficients,
    scorer_final_coefficients,
    pair_bias_weight,
    triangle_input_weight,
    triangle_output_gate,
    triangle_output_weight,
):
    sequence_local_rows = homolog_matrix.shape[0]
    residue_total = homolog_matrix.shape[1]
    alignment_width = homolog_matrix.shape[2]
    res_local = pair_state_input.shape[0]
    pair_width = pair_state_input.shape[2]
    opm_width = tensor_factor_coefficients.shape[1] // 2
    head_total = pair_bias_weight.shape[1]
    head_channel_width = alignment_width // head_total
    tri_width = triangle_input_weight.shape[1] // 4
    table_rows = relative_position_table.shape[0]
    row_start = lax.axis_index("row") * res_local
    contract = (((0,), (0,)), ((), ()))
    active_entry_mask = alignment_mask.astype(jnp.float32)
    homolog_rescaled = layer_normalize(homolog_matrix.astype(jnp.float32)).astype(jnp.bfloat16)
    homolog_lines_merged = homolog_rescaled.reshape(
        sequence_local_rows * residue_total, alignment_width
    )
    projected_rows = jnp.dot(
        homolog_lines_merged, tensor_factor_coefficients, preferred_element_type=jnp.float32
    ).reshape(sequence_local_rows, residue_total, 2 * opm_width)
    left_factor = (
        (projected_rows[..., :opm_width] * active_entry_mask[..., None])
        .astype(jnp.bfloat16)
        .reshape(sequence_local_rows, residue_total * opm_width)
    )
    right_factor = (
        (projected_rows[..., opm_width:] * active_entry_mask[..., None])
        .astype(jnp.bfloat16)
        .reshape(sequence_local_rows, residue_total * opm_width)
    )
    live_weights = active_entry_mask.astype(jnp.bfloat16)
    left_all, right_all, live_all = (
        lax.all_gather(left_factor, "row", axis=0, tiled=True),
        lax.all_gather(right_factor, "row", axis=0, tiled=True),
        lax.all_gather(live_weights, "row", axis=0, tiled=True),
    )
    left_cols = lax.dynamic_slice_in_dim(left_all, row_start * opm_width, res_local * opm_width, 1)
    live_cols = lax.dynamic_slice_in_dim(live_all, row_start, res_local, 1)
    outer_sum = lax.dot_general(left_cols, right_all, contract, preferred_element_type=jnp.float32)
    pair_count = lax.dot_general(live_cols, live_all, contract, preferred_element_type=jnp.float32)
    outer_flat = outer_sum.reshape(res_local, opm_width, residue_total, opm_width).transpose(
        0, 2, 1, 3
    )
    outer_flat = outer_flat.reshape(res_local * residue_total, opm_width * opm_width).astype(
        jnp.bfloat16
    )
    opm_update = jnp.dot(
        outer_flat, outer_output_weight, preferred_element_type=jnp.float32
    ).reshape(res_local, residue_total, pair_width)
    opm_update = opm_update / (0.001 + pair_count[..., None])
    chain_rows = lax.dynamic_slice_in_dim(chain_label, row_start, res_local, 0)
    index_rows = lax.dynamic_slice_in_dim(residue_number_index, row_start, res_local, 0)
    same_chain = chain_rows[:, None] == chain_label[None, :]
    offsets = (
        jnp.clip(index_rows[:, None] - residue_number_index[None, :], -REL_MAX, REL_MAX) + REL_MAX
    )
    bin_index = jnp.where(same_chain, offsets, 2 * REL_MAX + 1)
    one_hot = (
        (bin_index[..., None] == jnp.arange(table_rows, dtype=jnp.int32))
        .astype(jnp.float32)
        .reshape(-1, table_rows)
    )
    position_term = jnp.dot(
        one_hot, relative_position_table, precision=lax.Precision.HIGHEST
    ).reshape(res_local, residue_total, pair_width)
    updated = (pair_state_input.astype(jnp.float32) + position_term + opm_update).astype(
        jnp.bfloat16
    )
    pair_norm = layer_normalize(updated.astype(jnp.float32)).astype(jnp.bfloat16)
    pair_flat = pair_norm.reshape(res_local * residue_total, pair_width)
    head_bias = jnp.dot(pair_flat, pair_bias_weight, preferred_element_type=jnp.float32).astype(
        jnp.bfloat16
    )
    head_bias = head_bias.reshape(res_local, residue_total, head_total).transpose(2, 0, 1)
    full_bias = lax.all_gather(head_bias, "row", axis=1, tiled=True)
    tri_projected = jnp.dot(pair_flat, triangle_input_weight, preferred_element_type=jnp.float32)
    tri_left = (
        jax.nn.sigmoid(tri_projected[:, :tri_width]) * tri_projected[:, tri_width : 2 * tri_width]
    ).astype(jnp.bfloat16)
    tri_right = (
        jax.nn.sigmoid(tri_projected[:, 2 * tri_width : 3 * tri_width])
        * tri_projected[:, 3 * tri_width :]
    ).astype(jnp.bfloat16)
    tri_left = tri_left.reshape(res_local, residue_total, tri_width).transpose(2, 0, 1)
    tri_right = tri_right.reshape(res_local, residue_total, tri_width).transpose(2, 0, 1)
    left_channels, right_channels = (
        lax.all_to_all(tri_left, "row", split_axis=0, concat_axis=1, tiled=True),
        lax.all_to_all(tri_right, "row", split_axis=0, concat_axis=1, tiled=True),
    )
    channel_sum = jnp.einsum(
        "cki,ckj->cij", left_channels, right_channels, preferred_element_type=jnp.float32
    ).astype(jnp.bfloat16)
    row_sum = lax.all_to_all(channel_sum, "row", split_axis=1, concat_axis=0, tiled=True)
    tri_sum = row_sum.transpose(1, 2, 0)
    tri_normed = (
        layer_normalize(tri_sum.astype(jnp.float32))
        .astype(jnp.bfloat16)
        .reshape(res_local * residue_total, tri_width)
    )
    tri_gating = jax.nn.sigmoid(
        jnp.dot(pair_flat, triangle_output_gate, preferred_element_type=jnp.float32)
    )
    pair_state_output = updated.astype(jnp.float32).reshape(
        res_local * residue_total, pair_width
    ) + tri_gating * jnp.dot(tri_normed, triangle_output_weight, preferred_element_type=jnp.float32)
    pair_state_output = pair_state_output.astype(jnp.bfloat16).reshape(
        res_local, residue_total, pair_width
    )
    scorer_mapped_lines = jnp.dot(
        homolog_lines_merged, scorer_entry_coefficients, preferred_element_type=jnp.float32
    )
    asking_vectors = (
        scorer_mapped_lines[:, :alignment_width]
        .astype(jnp.bfloat16)
        .reshape(sequence_local_rows, residue_total, head_total, head_channel_width)
    )
    lookup_lines = (
        scorer_mapped_lines[:, alignment_width : 2 * alignment_width]
        .astype(jnp.bfloat16)
        .reshape(sequence_local_rows, residue_total, head_total, head_channel_width)
    )
    content_lines = (
        scorer_mapped_lines[:, 2 * alignment_width : 3 * alignment_width]
        .astype(jnp.bfloat16)
        .reshape(sequence_local_rows, residue_total, head_total, head_channel_width)
    )
    sigmoid_factor = (
        scorer_mapped_lines[:, 3 * alignment_width :]
        .astype(jnp.bfloat16)
        .reshape(sequence_local_rows, residue_total, head_total, head_channel_width)
    )
    mask_term = 1000000000.0 * (active_entry_mask - 1.0)
    score_scale = head_channel_width ** (-0.5)

    def attend(row_inputs):
        query_row, key_row, value_row, gate_row, mask_row = row_inputs
        scores = (
            jnp.einsum("ihd,jhd->hij", query_row, key_row, preferred_element_type=jnp.float32)
            * score_scale
        )
        scores = scores + full_bias.astype(jnp.float32) + mask_row[None, None, :]
        weights = jax.nn.softmax(scores, axis=-1).astype(jnp.bfloat16)
        attended = jnp.einsum(
            "hij,jhd->ihd", weights, value_row, preferred_element_type=jnp.float32
        )
        return (jax.nn.sigmoid(gate_row.astype(jnp.float32)) * attended).astype(jnp.bfloat16)

    sigmoid_scaled_lines = lax.map(
        attend, (asking_vectors, lookup_lines, content_lines, sigmoid_factor, mask_term)
    )
    homolog_revised = homolog_matrix.astype(jnp.float32).reshape(
        sequence_local_rows * residue_total, alignment_width
    ) + jnp.dot(
        sigmoid_scaled_lines.reshape(sequence_local_rows * residue_total, alignment_width),
        scorer_final_coefficients,
        preferred_element_type=jnp.float32,
    )
    homolog_revised = homolog_revised.astype(jnp.bfloat16).reshape(
        sequence_local_rows, residue_total, alignment_width
    )
    return (homolog_revised, pair_state_output)


def solution(mesh):
    n = mesh.shape["row"]

    def body(*blocks):
        msa, pair, w_out = blocks[0], blocks[2], blocks[13]
        rows, res, _ = msa.shape
        fits = (
            res == pair.shape[2] == w_out.shape[0] == 128
            and res % n == 0
            and w_out.shape[0] % n == 0
            and n % 8 == 0
            and rows == 2
            and (res // n) * (blocks[6].shape[1] // 2) == res
        )
        return fused_on_device(n, *blocks) if fits else on_device(*blocks)

    return jax.shard_map(
        body,
        mesh=mesh,
        in_specs=(
            P(("grp", "row"), None, None),
            P(("grp", "row"), None),
            P(("grp", "row"), None, None),
            P("grp"),
            P("grp"),
            P(),
            P(),
            P(),
            P(),
            P(),
            P(),
            P(),
            P(),
            P(),
        ),
        out_specs=(P(("grp", "row"), None, None), P(("grp", "row"), None, None)),
        check_vma=False,
    )
```

```python
import functools
import jax
import jax.numpy as jnp
from jax import lax
from jax.experimental import pallas as pl
from jax.experimental.pallas import tpu as pltpu
from jax.sharding import PartitionSpec as P

REL_MAX = 32
F32 = jnp.float32
BF16 = jnp.bfloat16
LEFT = jnp.bfloat16
OVER_FIRST = (((0,), (0,)), ((), ()))
OVER_LAST = (((1,), (1,)), ((), ()))


def mm(a, b):
    return jnp.dot(a, b, preferred_element_type=F32)


def norm_over(values, axis):
    centre = jnp.mean(values, axis=axis, keepdims=True)
    shifted = values - centre
    spread = jnp.mean(shifted * shifted, axis=axis, keepdims=True)
    return shifted * lax.rsqrt(spread + 1e-05)


def fused(
    n, *refs
):
    inputs, (msa_out, pair_out), landed = refs[:14], refs[14:16], refs[16:30]
    fused_body(n, inputs, landed, msa_out, pair_out, *refs[30:])


def fused_body(
    n, inputs, landed, msa_out, pair_out,
    left_send, left_recv, right_send, right_recv, tri_send, tri_recv, bias_send, bias_recv, sum_send, sum_recv,
    wide, outer_cat, w_outer_t, w_tri_t, base, qkvg, count, bias_wide, outer_wide, logits,
    send_sem, recv_sem, load_sem,
):
    msa, live_in, pair, chain, number, table, w_factor, w_outer, w_entry, w_final, w_bias, w_tri, w_gate, w_out = landed
    me = lax.axis_index("row")
    core = lax.rem(me, 2)
    chip = me // 2
    chips = n // 2
    sibling = me + 1 - 2 * core
    loads = [pltpu.make_async_copy(inputs[k], landed[k], load_sem.at[k]) for k in range(14)]
    for k in (0, 1, 6, 7, 8, 2, 11, 3, 4, 5, 12, 13, 9, 10):
        loads[k].start()
    rows, res, feats = msa.shape
    own, _, cz = pair.shape
    fac = w_factor.shape[0] // 2
    heads = w_bias.shape[0]
    span = feats // heads
    tri = w_out.shape[0]
    per = tri // n
    chunk = right_send.shape[0]

    barrier = pltpu.get_barrier_semaphore()

    def greet(t, _):
        pl.semaphore_signal(
            barrier, inc=1, device_id={"row": lax.rem(me + t, n)}, device_id_type=pl.DeviceIdType.MESH
        )
        return 0

    lax.fori_loop(1, n, greet, 0)

    def copy_to(phase, t, src, dst):
        return pltpu.make_async_remote_copy(
            src_ref=src,
            dst_ref=dst,
            send_sem=send_sem.at[phase, t],
            recv_sem=recv_sem.at[phase, me],
            device_id={"row": lax.rem(me + t, n)},
            device_id_type=pl.DeviceIdType.MESH,
        )

    def arrived(phase, t, src, dst):
        return pltpu.make_async_remote_copy(
            src_ref=src,
            dst_ref=dst,
            send_sem=send_sem.at[phase, t],
            recv_sem=recv_sem.at[phase, lax.rem(me + t, n)],
            device_id={"row": lax.rem(me + t, n)},
            device_id_type=pl.DeviceIdType.MESH,
        )

    for k in (0, 1, 6):
        loads[k].wait()
    live = live_in[...].astype(F32)
    factor_t = jnp.concatenate(
        [w_factor[...].astype(F32), jnp.zeros((2 * fac, feats), F32)], axis=0
    ).astype(BF16)
    normed = []
    base_row = n * chunk
    wide[base_row : base_row + 8 * n, :] = jnp.zeros((8 * n, res), F32)
    for s in range(rows):
        normed.append(norm_over(msa[s].astype(F32), 1).astype(BF16))
        factors = lax.dot_general(factor_t, normed[s], OVER_LAST, preferred_element_type=F32)
        factors = factors * live[s : s + 1, :]
        right_send[s * fac : (s + 1) * fac, :] = factors[fac : 2 * fac].astype(BF16)
        count[...] = jnp.transpose(
            jnp.concatenate([factors[0:fac], jnp.zeros((res - fac, res), F32)], axis=0)
        )
        packed = count[pl.ds(0, n, stride=own), :]
        for i in range(1, own):
            packed = packed + pltpu.roll(count[pl.ds(i, n, stride=own), :], i * fac, 1)
        wide[pl.ds(base_row + s, n, stride=8), :] = packed
        wide[pl.ds(base_row + rows + s, n, stride=8), :] = jnp.broadcast_to(live[s : s + 1, :], (n, res))
    left_send[...] = wide[base_row : base_row + 8 * n, :].astype(left_send.dtype).reshape(left_send.shape)

    pl.semaphore_wait(barrier, n - 1)

    def to_device(src, dst, out_sem, in_sem, device):
        return pltpu.make_async_remote_copy(
            src_ref=src, dst_ref=dst, send_sem=out_sem, recv_sem=in_sem,
            device_id={"row": device}, device_id_type=pl.DeviceIdType.MESH,
        )

    def right_out(t):
        to = lax.rem(chip + t, chips) * 2 + core
        return to_device(right_send, right_recv.at[me], send_sem.at[0, t], recv_sem.at[0, me], to)

    def right_on(t):
        frm = lax.rem(chip + chips - t, chips) * 2 + core
        return to_device(
            right_recv.at[frm], right_recv.at[frm], send_sem.at[0, chips + t], recv_sem.at[0, frm], sibling
        )

    def right_in(frm):
        return to_device(right_send, right_recv.at[frm], send_sem.at[0, 0], recv_sem.at[0, frm], sibling)

    def send_right(t, _):
        right_out(t).start()
        return 0

    def send_left(t, _):
        to = lax.rem(me + t, n)
        copy_to(1, t, left_send.at[to], left_recv.at[me]).start()
        return 0

    def widen_right(frm):
        wide[pl.ds(pl.multiple_of(frm * chunk, chunk), chunk), :] = right_recv[frm].astype(F32)

    def hand_on(t, _):
        frm = lax.rem(chip + chips - t, chips) * 2 + core
        right_in(frm).wait_recv()
        right_on(t).start()
        widen_right(frm)
        return 0

    lax.fori_loop(1, chips, send_right, 0)
    to_sibling = to_device(right_send, right_recv.at[me], send_sem.at[0, 0], recv_sem.at[0, me], sibling)
    to_sibling.start()
    lax.fori_loop(1, n, send_left, 0)
    right_recv[me] = right_send[...]
    widen_right(me)
    left_recv[me] = left_send[me]

    loads[7].wait()
    outer_wide[...] = w_outer[...].astype(F32)
    for e in range(fac):
        outer_cat[e * fac : (e + 1) * fac, 0:cz] = outer_wide[pl.ds(e, fac, stride=fac), :].astype(BF16)
    w_outer_t[...] = jnp.transpose(outer_cat[:, 0:cz].astype(F32)).astype(BF16)
    lax.fori_loop(1, 1 + chips // 4, hand_on, 0)
    for k in (8, 11, 12, 13):
        loads[k].wait()
    for b in range(4):
        w_tri_t[b * tri : (b + 1) * tri, :] = jnp.transpose(
            w_tri[:, b * tri : (b + 1) * tri].astype(F32)
        ).astype(BF16)
    gate_t = jnp.transpose(w_gate[...].astype(F32)).astype(BF16)
    out_t = jnp.transpose(w_out[...].astype(F32)).astype(BF16)
    for s in range(rows):
        qkvg[s] = mm(normed[s], w_entry[...]).astype(BF16)
    lax.fori_loop(1 + chips // 4, 1 + chips // 2, hand_on, 0)
    for k in (2, 3, 4, 5):
        loads[k].wait()
    lane = lax.broadcasted_iota(jnp.int32, (1, res), 1)
    bins = table.shape[0]
    padded = table.shape[0] + (-table.shape[0]) % 8
    slot = lax.broadcasted_iota(jnp.int32, (bins, res), 0).astype(F32)
    chain_row = chain[...].astype(F32)
    number_row = number[...].astype(F32)
    for i in range(own):
        mine = lane == me * own + i
        chain_i = jnp.sum(jnp.where(mine, chain_row, 0.0), axis=1, keepdims=True)
        number_i = jnp.sum(jnp.where(mine, number_row, 0.0), axis=1, keepdims=True)
        offset = jnp.clip(number_i - number_row, -float(REL_MAX), float(REL_MAX)) + float(REL_MAX)
        kind = jnp.where(chain_i == chain_row, offset, float(2 * REL_MAX + 1))
        hot = jnp.where(slot == kind, 1.0, 0.0)
        term = lax.dot_general(
            table[...], hot, OVER_FIRST, precision=lax.Precision.HIGHEST, preferred_element_type=F32
        )
        base[:, i * res : (i + 1) * res] = jnp.transpose(pair[i].astype(F32)) + term

    lax.fori_loop(1 + chips // 2, chips, hand_on, 0)

    def wait_left(t, _):
        frm = lax.rem(me + t, n)
        arrived(1, t, left_send.at[frm], left_recv.at[frm]).wait_recv()
        return 0

    def wait_sibling(t, _):
        frm = lax.rem(chip + chips - t, chips) * 2 + 1 - core
        right_in(frm).wait_recv()
        widen_right(frm)
        return 0

    lax.fori_loop(1, n, wait_left, 0)

    wide[base_row : base_row + 8 * n, :] = left_recv[...].astype(F32).reshape(8 * n, res)
    left_rows, live_rows = (
        jnp.concatenate([wide[pl.ds(base_row + r + s, n, stride=8), :] for s in range(rows)], axis=0)
        for r in (0, rows)
    )
    left_t = jnp.transpose(left_rows).astype(BF16)
    count[...] = mm(jnp.transpose(live_rows).astype(BF16), live_rows.astype(BF16))
    lax.fori_loop(0, chips, wait_sibling, 0)

    def right_at(k):
        return jnp.concatenate(
            [wide[pl.ds(s * fac + k, n, stride=chunk), :] for s in range(rows)], axis=0
        ).astype(BF16)

    for e in range(0, fac, 2):
        product = mm(left_t, jnp.concatenate([right_at(e), right_at(e + 1)], axis=1)).astype(BF16)
        for k in range(2):
            for i in range(own):
                outer_cat[(e + k) * fac : (e + k + 1) * fac, i * res : (i + 1) * res] = product[
                    i * fac : (i + 1) * fac, k * res : (k + 1) * res
                ]
    opm = mm(w_outer_t[...], outer_cat[...])
    for i in range(own):
        cols = slice(i * res, (i + 1) * res)
        base[:, cols] = base[:, cols] + opm[:, cols] * (1.0 / (0.001 + count[pl.ds(me * own + i, 1), :]))
    updated = base[...].astype(BF16).astype(F32)
    base[...] = updated
    pair_norm = norm_over(updated, 0).astype(BF16)

    projected = mm(w_tri_t[...], pair_norm)
    both = (
        jax.nn.sigmoid(projected[0:tri]) * projected[tri : 2 * tri],
        jax.nn.sigmoid(projected[2 * tri : 3 * tri]) * projected[3 * tri :],
    )
    lines = 2 * per * own
    for side in range(2):
        for c in range(per):
            for k in range(own):
                wide[pl.ds((side * per + c) * own + k, n, stride=lines), :] = both[side][
                    c * n : (c + 1) * n, k * res : (k + 1) * res
                ]
    tri_send[...] = wide[0 : n * lines, :].astype(BF16).reshape(tri_send.shape)
    def send_tri(t, _):
        to = lax.rem(me + t, n)
        copy_to(2, t, tri_send.at[to], tri_recv.at[me]).start()
        return 0

    def send_bias(t, _):
        copy_to(3, t, bias_send, bias_recv.at[me]).start()
        return 0

    lax.fori_loop(1, n, send_tri, 0)
    loads[10].wait()
    bias_t = mm(w_bias[...], pair_norm)
    bias_send[...] = jnp.concatenate(
        [bias_t[:, i * res : (i + 1) * res] for i in range(own)], axis=0
    ).astype(BF16)
    lax.fori_loop(1, n, send_bias, 0)
    tri_recv[me] = tri_send[me]
    bias_recv[me] = bias_send[...]
    gating = jax.nn.sigmoid(mm(gate_t, pair_norm))
    column = lax.broadcasted_iota(jnp.int32, (1, feats), 1)
    scale = span ** (-0.5)
    for s in range(rows):
        query = qkvg[s, :, 0:feats]
        key = qkvg[s, :, feats : 2 * feats]
        for h in range(heads):
            at_head = (column >= h * span) & (column < (h + 1) * span)
            scores = lax.dot_general(
                jnp.where(at_head, query, jnp.zeros_like(query)), key, OVER_LAST, preferred_element_type=F32
            )
            logits[s, h] = scores * scale

    def wait_tri(t, _):
        frm = lax.rem(me + t, n)
        arrived(2, t, tri_send.at[frm], tri_recv.at[frm]).wait_recv()
        return 0

    lax.fori_loop(1, n, wait_tri, 0)
    wide[0 : n * lines, :] = tri_recv[...].astype(F32).reshape(n * lines, res)
    sums = []
    for c in range(per):
        left_c, right_c = (
            jnp.concatenate(
                [wide[pl.ds((side * per + c) * own + k, n, stride=lines), :] for k in range(own)], axis=0
            )
            for side in range(2)
        )
        sums.append(mm(jnp.transpose(left_c).astype(BF16), right_c.astype(BF16)))
    for c in range(per):
        wide[pl.ds(c, res, stride=per), :] = sums[c]
    sum_send[...] = wide[0 : res * per, :].astype(BF16).reshape(sum_send.shape)

    def send_sum(t, _):
        to = lax.rem(me + t, n)
        copy_to(4, t, sum_send.at[to], sum_recv.at[me]).start()
        return 0

    lax.fori_loop(1, n, send_sum, 0)
    sum_recv[me] = sum_send[me]

    loads[9].wait()
    def wait_bias(t, _):
        frm = lax.rem(me + t, n)
        arrived(3, t, bias_send, bias_recv.at[frm]).wait_recv()
        return 0

    lax.fori_loop(1, n, wait_bias, 0)
    bias_wide[...] = bias_recv[...].astype(F32).reshape(bias_wide.shape)
    for s in range(rows):
        value = qkvg[s, :, 2 * feats : 3 * feats]
        gate = jax.nn.sigmoid(qkvg[s, :, 3 * feats :].astype(F32))
        mask = 1000000000.0 * (live[s : s + 1, :] - 1.0)
        attended = jnp.zeros((res, feats), F32)
        for h in range(heads):
            at_head = (column >= h * span) & (column < (h + 1) * span)
            scores = logits[s, h] + bias_wide[pl.ds(h, res, stride=heads), :] + mask
            scores = jnp.exp(scores - jnp.max(scores, axis=1, keepdims=True))
            weights = (scores * (1.0 / jnp.sum(scores, axis=1, keepdims=True))).astype(BF16)
            attended = jnp.where(at_head, mm(weights, value), attended)
        gated = (gate * attended).astype(BF16)
        msa_out[s] = (msa[s].astype(F32) + mm(gated, w_final[...])).astype(BF16)

    def wait_sum(t, _):
        frm = lax.rem(me + t, n)
        arrived(4, t, sum_send.at[frm], sum_recv.at[frm]).wait_recv()
        return 0

    lax.fori_loop(1, n, wait_sum, 0)
    wide[0 : res * per, :] = sum_recv[...].astype(F32).reshape(res * per, res)
    for i in range(own):
        tri_sum = jnp.concatenate(
            [wide[pl.ds(i * per + c, n, stride=own * per), :] for c in range(per)], axis=0
        )
        tri_normed = norm_over(tri_sum, 0).astype(BF16)
        cols = slice(i * res, (i + 1) * res)
        result = base[:, cols] + gating[:, cols] * mm(out_t, tri_normed)
        pair_out[i] = jnp.transpose(result).astype(BF16)

    def all_sent(t, _):
        to = lax.rem(me + t, n)
        copy_to(1, t, left_send.at[to], left_recv.at[me]).wait_send()
        copy_to(2, t, tri_send.at[to], tri_recv.at[me]).wait_send()
        copy_to(3, t, bias_send, bias_recv.at[me]).wait_send()
        copy_to(4, t, sum_send.at[to], sum_recv.at[me]).wait_send()
        return 0

    def right_sent(t, _):
        right_out(t).wait_send()
        right_on(t).wait_send()
        return 0

    lax.fori_loop(1, n, all_sent, 0)
    lax.fori_loop(1, chips, right_sent, 0)
    to_sibling.wait_send()


def fused_on_device(
    n, msa, live, pair, chain, number, table, w_factor, w_outer, w_entry, w_final, w_bias, w_tri, w_gate, w_out
):
    rows, res, feats = msa.shape
    own, _, cz = pair.shape
    fac = w_factor.shape[1] // 2
    heads = w_bias.shape[1]
    tri = w_out.shape[0]
    per = tri // n
    chunk = rows * fac
    lines = 2 * per * own
    wide_rows = max(n * chunk + 8 * n, n * lines, per * res)
    vmem = pl.BlockSpec(memory_space=pltpu.VMEM)
    args = (
        msa, live, pair, chain.reshape(1, res), number.reshape(1, res), table,
        w_factor.T, w_outer, w_entry, w_final, w_bias.T, w_tri, w_gate, w_out,
    )
    return pl.pallas_call(
        functools.partial(fused, n),
        out_shape=(jax.ShapeDtypeStruct(msa.shape, BF16), jax.ShapeDtypeStruct(pair.shape, BF16)),
        in_specs=[pl.BlockSpec(memory_space=pltpu.HBM)] * 14,
        out_specs=(vmem, vmem),
        scratch_shapes=[
            *[pltpu.VMEM(a.shape, a.dtype) for a in args],
            pltpu.VMEM((n, 8, res), LEFT),
            pltpu.VMEM((n, 8, res), LEFT),
            pltpu.VMEM((chunk, res), BF16),
            pltpu.VMEM((n, chunk, res), BF16),
            pltpu.VMEM((n, lines, res), BF16),
            pltpu.VMEM((n, lines, res), BF16),
            pltpu.VMEM((own * heads, res), BF16),
            pltpu.VMEM((n, own * heads, res), BF16),
            pltpu.VMEM((n, own * per, res), BF16),
            pltpu.VMEM((n, own * per, res), BF16),
            pltpu.VMEM((wide_rows, res), F32),
            pltpu.VMEM((fac * fac, own * res), BF16),
            pltpu.VMEM((cz, fac * fac), BF16),
            pltpu.VMEM((4 * tri, cz), BF16),
            pltpu.VMEM((cz, own * res), F32),
            pltpu.VMEM((rows, res, 4 * feats), BF16),
            pltpu.VMEM((res, res), F32),
            pltpu.VMEM((n * own * heads, res), F32),
            pltpu.VMEM((fac * fac, cz), F32),
            pltpu.VMEM((rows, heads, res, res), F32),
            pltpu.SemaphoreType.DMA((5, n)),
            pltpu.SemaphoreType.DMA((5, n)),
            pltpu.SemaphoreType.DMA((14,)),
        ],
        compiler_params=pltpu.CompilerParams(
            collective_id=0, has_side_effects=True, vmem_limit_bytes=64 * 1024 * 1024 - 4096
        ),
    )(*args)


def layer_normalize(values):
    centre = jnp.mean(values, axis=-1, keepdims=True)
    shifted = values - centre
    spread = jnp.mean(shifted * shifted, axis=-1, keepdims=True)
    return shifted * lax.rsqrt(spread + 1e-05)


def on_device(
    homolog_matrix,
    alignment_mask,
    pair_state_input,
    chain_label,
    residue_number_index,
    relative_position_table,
    tensor_factor_coefficients,
    outer_output_weight,
    scorer_entry_coefficients,
    scorer_final_coefficients,
    pair_bias_weight,
    triangle_input_weight,
    triangle_output_gate,
    triangle_output_weight,
):
    sequence_local_rows = homolog_matrix.shape[0]
    residue_total = homolog_matrix.shape[1]
    alignment_width = homolog_matrix.shape[2]
    res_local = pair_state_input.shape[0]
    pair_width = pair_state_input.shape[2]
    opm_width = tensor_factor_coefficients.shape[1] // 2
    head_total = pair_bias_weight.shape[1]
    head_channel_width = alignment_width // head_total
    tri_width = triangle_input_weight.shape[1] // 4
    table_rows = relative_position_table.shape[0]
    row_start = lax.axis_index("row") * res_local
    contract = (((0,), (0,)), ((), ()))
    active_entry_mask = alignment_mask.astype(jnp.float32)
    homolog_rescaled = layer_normalize(homolog_matrix.astype(jnp.float32)).astype(jnp.bfloat16)
    homolog_lines_merged = homolog_rescaled.reshape(
        sequence_local_rows * residue_total, alignment_width
    )
    projected_rows = jnp.dot(
        homolog_lines_merged, tensor_factor_coefficients, preferred_element_type=jnp.float32
    ).reshape(sequence_local_rows, residue_total, 2 * opm_width)
    left_factor = (
        (projected_rows[..., :opm_width] * active_entry_mask[..., None])
        .astype(jnp.bfloat16)
        .reshape(sequence_local_rows, residue_total * opm_width)
    )
    right_factor = (
        (projected_rows[..., opm_width:] * active_entry_mask[..., None])
        .astype(jnp.bfloat16)
        .reshape(sequence_local_rows, residue_total * opm_width)
    )
    live_weights = active_entry_mask.astype(jnp.bfloat16)
    left_all, right_all, live_all = (
        lax.all_gather(left_factor, "row", axis=0, tiled=True),
        lax.all_gather(right_factor, "row", axis=0, tiled=True),
        lax.all_gather(live_weights, "row", axis=0, tiled=True),
    )
    left_cols = lax.dynamic_slice_in_dim(left_all, row_start * opm_width, res_local * opm_width, 1)
    live_cols = lax.dynamic_slice_in_dim(live_all, row_start, res_local, 1)
    outer_sum = lax.dot_general(left_cols, right_all, contract, preferred_element_type=jnp.float32)
    pair_count = lax.dot_general(live_cols, live_all, contract, preferred_element_type=jnp.float32)
    outer_flat = outer_sum.reshape(res_local, opm_width, residue_total, opm_width).transpose(
        0, 2, 1, 3
    )
    outer_flat = outer_flat.reshape(res_local * residue_total, opm_width * opm_width).astype(
        jnp.bfloat16
    )
    opm_update = jnp.dot(
        outer_flat, outer_output_weight, preferred_element_type=jnp.float32
    ).reshape(res_local, residue_total, pair_width)
    opm_update = opm_update / (0.001 + pair_count[..., None])
    chain_rows = lax.dynamic_slice_in_dim(chain_label, row_start, res_local, 0)
    index_rows = lax.dynamic_slice_in_dim(residue_number_index, row_start, res_local, 0)
    same_chain = chain_rows[:, None] == chain_label[None, :]
    offsets = (
        jnp.clip(index_rows[:, None] - residue_number_index[None, :], -REL_MAX, REL_MAX) + REL_MAX
    )
    bin_index = jnp.where(same_chain, offsets, 2 * REL_MAX + 1)
    one_hot = (
        (bin_index[..., None] == jnp.arange(table_rows, dtype=jnp.int32))
        .astype(jnp.float32)
        .reshape(-1, table_rows)
    )
    position_term = jnp.dot(
        one_hot, relative_position_table, precision=lax.Precision.HIGHEST
    ).reshape(res_local, residue_total, pair_width)
    updated = (pair_state_input.astype(jnp.float32) + position_term + opm_update).astype(
        jnp.bfloat16
    )
    pair_norm = layer_normalize(updated.astype(jnp.float32)).astype(jnp.bfloat16)
    pair_flat = pair_norm.reshape(res_local * residue_total, pair_width)
    head_bias = jnp.dot(pair_flat, pair_bias_weight, preferred_element_type=jnp.float32).astype(
        jnp.bfloat16
    )
    head_bias = head_bias.reshape(res_local, residue_total, head_total).transpose(2, 0, 1)
    full_bias = lax.all_gather(head_bias, "row", axis=1, tiled=True)
    tri_projected = jnp.dot(pair_flat, triangle_input_weight, preferred_element_type=jnp.float32)
    tri_left = (
        jax.nn.sigmoid(tri_projected[:, :tri_width]) * tri_projected[:, tri_width : 2 * tri_width]
    ).astype(jnp.bfloat16)
    tri_right = (
        jax.nn.sigmoid(tri_projected[:, 2 * tri_width : 3 * tri_width])
        * tri_projected[:, 3 * tri_width :]
    ).astype(jnp.bfloat16)
    tri_left = tri_left.reshape(res_local, residue_total, tri_width).transpose(2, 0, 1)
    tri_right = tri_right.reshape(res_local, residue_total, tri_width).transpose(2, 0, 1)
    left_channels, right_channels = (
        lax.all_to_all(tri_left, "row", split_axis=0, concat_axis=1, tiled=True),
        lax.all_to_all(tri_right, "row", split_axis=0, concat_axis=1, tiled=True),
    )
    channel_sum = jnp.einsum(
        "cki,ckj->cij", left_channels, right_channels, preferred_element_type=jnp.float32
    ).astype(jnp.bfloat16)
    row_sum = lax.all_to_all(channel_sum, "row", split_axis=1, concat_axis=0, tiled=True)
    tri_sum = row_sum.transpose(1, 2, 0)
    tri_normed = (
        layer_normalize(tri_sum.astype(jnp.float32))
        .astype(jnp.bfloat16)
        .reshape(res_local * residue_total, tri_width)
    )
    tri_gating = jax.nn.sigmoid(
        jnp.dot(pair_flat, triangle_output_gate, preferred_element_type=jnp.float32)
    )
    pair_state_output = updated.astype(jnp.float32).reshape(
        res_local * residue_total, pair_width
    ) + tri_gating * jnp.dot(tri_normed, triangle_output_weight, preferred_element_type=jnp.float32)
    pair_state_output = pair_state_output.astype(jnp.bfloat16).reshape(
        res_local, residue_total, pair_width
    )
    scorer_mapped_lines = jnp.dot(
        homolog_lines_merged, scorer_entry_coefficients, preferred_element_type=jnp.float32
    )
    asking_vectors = (
        scorer_mapped_lines[:, :alignment_width]
        .astype(jnp.bfloat16)
        .reshape(sequence_local_rows, residue_total, head_total, head_channel_width)
    )
    lookup_lines = (
        scorer_mapped_lines[:, alignment_width : 2 * alignment_width]
        .astype(jnp.bfloat16)
        .reshape(sequence_local_rows, residue_total, head_total, head_channel_width)
    )
    content_lines = (
        scorer_mapped_lines[:, 2 * alignment_width : 3 * alignment_width]
        .astype(jnp.bfloat16)
        .reshape(sequence_local_rows, residue_total, head_total, head_channel_width)
    )
    sigmoid_factor = (
        scorer_mapped_lines[:, 3 * alignment_width :]
        .astype(jnp.bfloat16)
        .reshape(sequence_local_rows, residue_total, head_total, head_channel_width)
    )
    mask_term = 1000000000.0 * (active_entry_mask - 1.0)
    score_scale = head_channel_width ** (-0.5)

    def attend(row_inputs):
        query_row, key_row, value_row, gate_row, mask_row = row_inputs
        scores = (
            jnp.einsum("ihd,jhd->hij", query_row, key_row, preferred_element_type=jnp.float32)
            * score_scale
        )
        scores = scores + full_bias.astype(jnp.float32) + mask_row[None, None, :]
        weights = jax.nn.softmax(scores, axis=-1).astype(jnp.bfloat16)
        attended = jnp.einsum(
            "hij,jhd->ihd", weights, value_row, preferred_element_type=jnp.float32
        )
        return (jax.nn.sigmoid(gate_row.astype(jnp.float32)) * attended).astype(jnp.bfloat16)

    sigmoid_scaled_lines = lax.map(
        attend, (asking_vectors, lookup_lines, content_lines, sigmoid_factor, mask_term)
    )
    homolog_revised = homolog_matrix.astype(jnp.float32).reshape(
        sequence_local_rows * residue_total, alignment_width
    ) + jnp.dot(
        sigmoid_scaled_lines.reshape(sequence_local_rows * residue_total, alignment_width),
        scorer_final_coefficients,
        preferred_element_type=jnp.float32,
    )
    homolog_revised = homolog_revised.astype(jnp.bfloat16).reshape(
        sequence_local_rows, residue_total, alignment_width
    )
    return (homolog_revised, pair_state_output)


def solution(mesh):
    n = mesh.shape["row"]

    def body(*blocks):
        msa, pair, w_out = blocks[0], blocks[2], blocks[13]
        rows, res, _ = msa.shape
        fits = (
            res == pair.shape[2] == w_out.shape[0] == 128
            and res % n == 0
            and w_out.shape[0] % n == 0
            and n % 8 == 0
            and rows == 2
            and (res // n) * (blocks[6].shape[1] // 2) == res
        )
        return fused_on_device(n, *blocks) if fits else on_device(*blocks)

    return jax.shard_map(
        body,
        mesh=mesh,
        in_specs=(
            P(("grp", "row"), None, None),
            P(("grp", "row"), None),
            P(("grp", "row"), None, None),
            P("grp"),
            P("grp"),
            P(),
            P(),
            P(),
            P(),
            P(),
            P(),
            P(),
            P(),
            P(),
        ),
        out_specs=(P(("grp", "row"), None, None), P(("grp", "row"), None, None)),
        check_vma=False,
    )
```
